32 devices in a mesh: leaf: 32 (over z, y, x, core).
Axes of the slice: x: 2, y: 2, z: 4, core: 2. Of those that a mesh axis runs over, the one named last changes fastest.
Arguments:
- points: bfloat16 [64, 32768], P(None, 'leaf'), may hold values from -6 to 6
- weights: bfloat16 [32768, 512], P('leaf'), may hold values from -1.1953125 to 1.1953125
- interp: bfloat16 [32768, 512], P('leaf'), may hold values from -0.1875 to 0.1875
- transfers: bfloat16 [32, 5, 512, 512], P('leaf'), may hold values from -0.25 to 0.25
- near_mask: int32 [32, 4], P('leaf'), may hold values 0 or 1
- skel_index: int32 [32, 512], P('leaf'), may hold values from 0 to 1023, as said below
Outputs:
- product: bfloat16 [32768, 512], P('leaf')
The draws below stay inside these ranges and needn't reach their ends.
Inputs may be any that keep to these rules, and one draw needn't show every extreme that they name: `skel_index`: each row holds 512 distinct ranks.
All inputs are finite; a program needn't handle non-finite values. No bound on the sum of `near_mask` on one device may be relied on, other than what follows from the above.
Results may differ from the reference program's by a relative error of at most 0.0075.
Values may be sent and summed in bfloat16 or wider, within the bound.
A program may use at most 128 MiB of HBM per device.

```python
import jax
import jax.numpy as jnp
from jax import lax

DIM = 64
RHS = 512
S = 512
NPTS = 1024
LEVELS = 5
RADIUS = 2
LEAVES = 32
POINTS = 32768


def pick_row(row_key):
    return jax.random.permutation(row_key, NPTS)[:S]


def draw_skel_index(key, part):
    row_keys = jax.random.split(jax.random.fold_in(key, 17), LEAVES)
    return jax.vmap(pick_row)(row_keys).astype(jnp.int32)


def set_ends(array, stream_key, low, largest):
    index_at = [jax.random.randint(jax.random.fold_in(stream_key, axis), (), 0, length) for axis, length in enumerate(array.shape)]
    widest = array.shape.index(max(array.shape))
    next_to = index_at[:widest] + [(index_at[widest] + 1) % array.shape[widest]] + index_at[widest + 1:]
    return array.at[tuple(index_at)].set(low).at[tuple(next_to)].set(largest)


def levels(stream_key, extent, shards, smallest, top_value):
    def one(axis_at, parts):
        steps = jax.random.uniform(jax.random.fold_in(jax.random.fold_in(stream_key, 6), axis_at), (parts,), jnp.float32, smallest / len(shards), top_value / len(shards))
        return jnp.repeat(jnp.exp(steps), extent[axis_at] // parts).reshape((-1,) + (1,) * (len(extent) - axis_at - 1))

    factor_of = one(*shards[0])
    for cut in shards[1:]:
        factor_of = factor_of * one(*cut)
    return factor_of


def centred(own_key, shape, deviation, most, cuts=(), held_as=jnp.bfloat16):
    gain = levels(own_key, shape, cuts, -0.22, 0.18) if cuts else 1.0
    drawn = jax.random.normal(own_key, shape, jnp.float32) * deviation * gain
    return jnp.minimum(jnp.maximum(drawn, -most), most).astype(held_as)


def setup_inputs(seed: int = 0) -> dict:
    streams_of = jax.random.split(jax.random.key(seed), 7)
    return {
        "points": centred(streams_of[0], (DIM, POINTS), 1.0, 6.0, ((1, 32),)),
        "weights": centred(streams_of[1], (POINTS, RHS), 0.2, 1.1953125, ((0, 32),)),
        "interp": centred(streams_of[2], (POINTS, S), NPTS ** -0.5, 0.1875, ((0, 32),)),
        "transfers": centred(streams_of[3], (LEAVES, LEVELS, S, S), S ** -0.5, 0.25, ((0, 32),)),
        "near_mask": set_ends((jax.random.randint(streams_of[4], (LEAVES, 2 * RADIUS), 0, 4) < 3).astype(jnp.int32), jax.random.fold_in(streams_of[4], 1), 0, 1),
        "skel_index": draw_skel_index(jax.random.fold_in(streams_of[6], 71), 0),
    }


def widened(value):
    return lax.optimization_barrier(value).astype(jnp.float32)


def kernel_tile(left, right):
    left_wide = left.astype(jnp.float32)
    right_wide = right.astype(jnp.float32)
    sq_left = jnp.sum(left_wide * left_wide, axis=0)
    sq_right = jnp.sum(right_wide * right_wide, axis=0)
    cross_terms = lax.dot_general(left, right, (((0,), (0,)), ((), ())), preferred_element_type=jnp.float32)
    distance = sq_left[:, None] + sq_right[None, :] - 2.0 * cross_terms
    return jnp.exp(distance * (-1.0 / DIM)).astype(jnp.bfloat16)


def reference(points, weights, interp, transfers, near_mask, skel_index):
    leaf_points = points.reshape(DIM, LEAVES, NPTS).transpose(1, 0, 2)
    leaf_weights_in = weights.reshape(LEAVES, NPTS, RHS)
    leaf_interp = interp.reshape(LEAVES, NPTS, S)
    offsets = list(range(-RADIUS, 0)) + list(range(1, RADIUS + 1))

    def near_leaf(leaf_id):
        own_points = leaf_points[leaf_id]
        total = jnp.dot(kernel_tile(own_points, own_points), leaf_weights_in[leaf_id], preferred_element_type=jnp.float32)
        for slot_index, offset in enumerate(offsets):
            target = leaf_id + offset
            neighbour = jnp.clip(target, 0, LEAVES - 1)
            in_range = (target >= 0) & (target < LEAVES)
            flag_value = jnp.where(in_range, near_mask[leaf_id, slot_index], 0).astype(jnp.float32)
            block = jnp.dot(kernel_tile(own_points, leaf_points[neighbour]), leaf_weights_in[neighbour], preferred_element_type=jnp.float32)
            total = total + flag_value * block
        return total

    leaf_ids = jnp.arange(LEAVES, dtype=jnp.int32)
    near_field = lax.map(near_leaf, leaf_ids)
    skel_points = jnp.take_along_axis(leaf_points, skel_index[:, None, :], axis=2)
    leaf_weights = jnp.einsum("nps,npr->nsr", widened(leaf_interp), widened(leaf_weights_in)).astype(jnp.bfloat16)
    far_sum = jnp.zeros((LEAVES, S, RHS), jnp.float32)
    for level in range(LEVELS):
        transfer_level = widened(transfers[:, level])
        level_terms = jnp.einsum("nab,nar->nbr", transfer_level, widened(leaf_weights))
        nodes = LEAVES >> level
        group = 2 ** level
        node_sums = level_terms.reshape(nodes, group, S, RHS).sum(axis=1).astype(jnp.bfloat16)
        columns_kept = S >> level
        node_points = skel_points[:, :, :columns_kept].reshape(nodes, group, DIM, columns_kept)
        node_points = node_points.transpose(0, 2, 1, 3).reshape(nodes, DIM, S)

        def couple_node(node_id):
            partner = node_id ^ 1
            tile = kernel_tile(node_points[node_id], node_points[partner])
            return jnp.dot(tile, node_sums[partner], preferred_element_type=jnp.float32).astype(jnp.bfloat16)

        coupled = lax.map(couple_node, jnp.arange(nodes, dtype=jnp.int32))
        coupled_leaf = jnp.repeat(coupled, group, axis=0)
        far_sum = far_sum + jnp.einsum("nab,nbr->nar", transfer_level, widened(coupled_leaf))
    far_skeleton = far_sum.astype(jnp.bfloat16)
    far_field = jnp.einsum("nps,nsr->npr", widened(leaf_interp), widened(far_skeleton))
    return (near_field + far_field).astype(jnp.bfloat16).reshape(POINTS, RHS)
```

```python
import functools
import math

import jax
import jax.numpy as jnp
from jax import lax
from jax.experimental import pallas as pl
from jax.experimental.pallas import tpu as pltpu
from jax.sharding import PartitionSpec as P

MESH = pl.DeviceIdType.MESH
LANES = 128
CHUNKS = 8
LAG = 3
F32, BF16 = jnp.float32, jnp.bfloat16


def rounded(value):
    return value.astype(BF16).astype(F32)


def dot(left, right, dims=((1,), (0,))):
    return lax.dot_general(left, right, (dims, ((), ())), preferred_element_type=F32)


def left_form(wide, dim):
    lane = lax.broadcasted_iota(jnp.int32, wide.shape, 1)
    norm = jnp.sum(jnp.where((lane >= dim) & (lane < dim + 3), wide, 0.0), axis=1, keepdims=True)
    left = jnp.where(lane < dim, 2.0 * wide, jnp.where(lane < dim + 3, -1.0, 0.0))
    return left.astype(BF16), norm


def reduce_bits(level):
    return list(range(level - 1, 0, -1))


def plan(levels):
    names = []
    for level in range(levels):
        for bit in reduce_bits(level):
            names += [("rs", level, bit), ("ag", level, bit)]
        names += [("rs0", level), ("ag0", level), ("ex", level), ("pt", level), ("pt0", level)]
    names += [("own", 0), ("own", 1)]
    for chunk in range(CHUNKS + 1):
        for leaf in range(2):
            names += [("bx", leaf, chunk), ("fw", leaf, chunk)]
        names += [("bm", slot, chunk) for slot in range(4)]
    return {name: at for at, name in enumerate(names)}


def body(
    count, slots,
    pts, w, interp, trans, mask, index,
    out,
    rown, lown, nown, rbuf, wbuf, near, lw, keep, tx, rx, mx, sib, pbuf, psib, far,
    send_sem, recv_sem,
):
    me = lax.axis_index("leaf")
    core, chip = lax.rem(me, 2), lax.rem(me // 2, 2)
    even = chip == 0
    dim, npts = pts.shape
    rank, rhs = lw.shape
    half = rank // 2
    levels = trans.shape[0]
    deep = rown.shape[0]
    scale = math.log2(math.e) / dim

    def partner(bit):
        on = lax.rem(me // (1 << bit), 2)
        return me + (1 - 2 * on) * (1 << bit), on

    mate, xmate = partner(0)[0], partner(1)[0]
    ahead = me + 4 * (1 - 2 * chip)
    behind = me - 4 * (1 - 2 * chip)
    has_ahead = (ahead >= 0) & (ahead < count)
    has_behind = (behind >= 0) & (behind < count)

    def copy(name, src, dst, device):
        at = slots[name]
        return pltpu.make_async_remote_copy(
            src_ref=src, dst_ref=dst, send_sem=send_sem.at[at], recv_sem=recv_sem.at[at],
            device_id=(device,), device_id_type=MESH,
        )

    barrier = pltpu.get_barrier_semaphore()
    for bit in range(levels):
        pl.semaphore_signal(barrier, inc=1, device_id=(partner(bit)[0],), device_id_type=MESH)
    for other, there in ((ahead, has_ahead), (behind, has_behind)):
        @pl.when(there)
        def _():
            pl.semaphore_signal(barrier, inc=1, device_id=(other,), device_id_type=MESH)

    wide = pts[...].astype(F32)
    norm = jnp.sum(wide * wide, axis=0, keepdims=True)
    high = rounded(norm)
    middle = rounded(norm - high)
    low = norm - high - middle
    row = lax.broadcasted_iota(jnp.int32, (LANES - dim, npts), 0)
    extra = jnp.where(row == 0, high, jnp.where(row == 1, middle, jnp.where(row == 2, low, 0.0)))
    full = jnp.concatenate([wide, extra], axis=0)
    rown[...] = full[:deep].astype(BF16)

    pl.semaphore_wait(barrier, levels + has_ahead.astype(jnp.int32) + has_behind.astype(jnp.int32))

    step = npts // CHUNKS

    def part(chunk):
        return pl.ds((chunk - 1) * step, step)

    def own(which):
        if which == 0:
            return copy(("own", 0), rown, rbuf.at[4], mate)
        return copy(("own", 1), w, wbuf.at[4], mate)

    def between(name, src, dst, chunk, device):
        if chunk == 0:
            return copy(name, src[0], dst[0], device)
        return copy(name, src[1].at[part(chunk)], dst[1].at[part(chunk)], device)

    def leaf_slot(slot):
        return rbuf.at[slot], wbuf.at[slot]

    def to_x(leaf, chunk):
        source = (rown, w) if leaf == 0 else leaf_slot(4)
        return between(("bx", leaf, chunk), source, leaf_slot(leaf), chunk, xmate)

    def forward(leaf, chunk):
        return between(("fw", leaf, chunk), leaf_slot(leaf), leaf_slot(2 + leaf), chunk, ahead)

    def to_mate(slot, chunk):
        return between(("bm", slot, chunk), leaf_slot(slot), leaf_slot(slot), chunk, mate)

    chunks = range(CHUNKS + 1)

    own(1).start()
    own(0).start()

    @pl.when(core == 0)
    def _():
        for chunk in chunks:
            to_x(0, chunk).start()

    left, norm_column = left_form(jnp.transpose(full), dim)
    lown[...] = left
    nown[...] = norm_column
    chosen = (lax.broadcasted_iota(jnp.int32, (npts, rank), 0) == index[...]).astype(BF16)
    pbuf[0] = jnp.transpose(dot(full.astype(BF16), chosen)).astype(BF16)

    def points_copy(level):
        return copy(("pt", level), pbuf.at[level], psib.at[level], partner(level)[0])

    def points_mate(level):
        return copy(("pt0", level), psib.at[level], psib.at[level], mate)

    def points_join(level):
        if level + 1 == levels:
            return
        group, width = 1 << level, rank >> level

        def halved(ref):
            return ref[level].reshape(group, width, LANES)[:, : width // 2].reshape(rank // 2, LANES)

        mine, theirs = halved(pbuf), halved(psib)
        upper = partner(level)[1] == 1
        pbuf[level + 1, : rank // 2] = jnp.where(upper, theirs, mine)
        pbuf[level + 1, rank // 2 :] = jnp.where(upper, mine, theirs)

    points_copy(0).start()

    lw[...] = dot(interp[...], w[...], ((0,), (0,))).astype(BF16)
    kept_at = pl.multiple_of(core * half, half)
    sent_at = pl.multiple_of((1 - core) * half, half)

    def geometry(level, upto):
        bits = reduce_bits(level)
        offset, length = 0, rank
        for bit in bits[:upto]:
            length //= 2
            offset = offset + partner(bit)[1] * length
        if upto:
            offset = pl.multiple_of(offset, length)
        return offset, length

    def term_copy(level):
        if level == 1:
            return copy(("rs0", 1), tx.at[1, pl.ds(0, half)], mx.at[1, pl.ds(0, half)], mate)
        return copy(("rs0", level), tx.at[level], mx.at[level], mate)

    def reduce_copy(level, at):
        bit = reduce_bits(level)[at]
        length = rank >> (at + 1)
        rows = pl.ds(rank - 2 * length, length)
        return copy(("rs", level, bit), tx.at[level, rows], rx.at[level, rows], partner(bit)[0])

    def exchange_copy(level):
        if level == 0:
            return copy(("ex", 0), tx.at[0], sib.at[0], mate)
        if level == 1:
            return copy(("ex", 1), tx.at[1, pl.ds(half, half)], sib.at[1, pl.ds(kept_at, half)], xmate)
        offset, length = geometry(level, level - 1)
        rows = pl.ds(rank - length, length)
        return copy(("ex", level), tx.at[level, rows], sib.at[level, pl.ds(offset, length)], partner(level)[0])

    def gather_copy(level, at):
        bit = reduce_bits(level)[at]
        offset, length = geometry(level, at + 1)
        rows = pl.ds(offset, length)
        return copy(("ag", level, bit), sib.at[level, rows], sib.at[level, rows], partner(bit)[0])

    def share_copy(level):
        if level == 1:
            rows = pl.ds(kept_at, half)
            return copy(("ag0", 1), sib.at[1, rows], sib.at[1, rows], mate)
        return copy(("ag0", level), sib.at[level], sib.at[level], mate)

    def term(level, rows=None):
        block = trans[level] if rows is None else trans[level, :, rows]
        return dot(block, lw[...], ((0,), (0,)))

    block = 256
    tiles = npts // block

    def near_part(right, weights, flag, first=0, last=tiles):
        @pl.loop(first, last)
        def _(at):
            rows = pl.ds(pl.multiple_of(at * block, block), block)
            power = dot(lown[rows, :deep], right[...]) - nown[rows]
            tile = jnp.exp2(power * scale).astype(BF16)
            value = dot(tile, weights[...])
            near[rows] = value if flag is None else near[rows] + flag.astype(F32) * value

    def near_self(first, last):
        near_part(rown, w, None, first, last)

    def near_slot(slot, flag, first=0, last=tiles):
        near_part(rbuf.at[slot], wbuf.at[slot], flag, first, last)

    def couple(level):
        left, norm_own = left_form(pbuf[level].astype(F32), dim)
        power = dot(left, psib[level], ((1,), (1,))) - norm_own
        tile = jnp.exp2(power * scale).astype(BF16)
        coupled = dot(tile, sib[level]).astype(BF16)
        value = dot(trans[level], coupled)
        far[...] = value if level == 0 else far[...] + value

    def level_one_ready():
        term_copy(1).wait_recv()
        tx[1, half:] = (keep[1, :half] + mx[1, :half].astype(F32)).astype(BF16)

    def level_zero_and_one():
        tx[1, :half] = term(1, pl.ds(sent_at, half)).astype(BF16)
        term_copy(1).start()
        keep[1, :half] = term(1, pl.ds(kept_at, half))
        tx[0] = term(0).astype(BF16)
        exchange_copy(0).start()

    @pl.when(core == 0)
    def _():
        for level in range(levels - 1, 1, -1):
            tx[level] = term(level).astype(BF16)
            term_copy(level).start()
        own(1).wait_recv()
        own(0).wait_recv()
        for chunk in chunks:
            to_x(1, chunk).start()
        level_zero_and_one()
        level_one_ready()
        exchange_copy(1).start()
        points_copy(0).wait()
        points_join(0)

        flags = [
            jnp.where(even, mask[0, 3], mask[0, 0]),
            jnp.where(even, mask[0, 0], mask[0, 3]),
            mask[0, 1],
        ]
        third = jnp.where(even, 3, 1)

        def relay(at):
            leaf, chunk = divmod(at, CHUNKS + 1)
            to_x(leaf, chunk).wait_recv()

            @pl.when(has_ahead)
            def _():
                forward(leaf, chunk).start()

            if leaf == 1:
                to_mate(1, chunk).start()
            else:
                @pl.when(even)
                def _():
                    to_mate(0, chunk).start()

        def collect(at):
            leaf, chunk = divmod(at, CHUNKS + 1)

            @pl.when(has_behind)
            def _():
                forward(leaf, chunk).wait_recv()
                if leaf == 1:
                    to_mate(3, chunk).start()

            if leaf == 0:
                @pl.when(has_behind & jnp.logical_not(even))
                def _():
                    to_mate(2, chunk).start()

        def points_here(level):
            points_mate(level).wait_recv()
            points_join(level)

        def far_level(level):
            share_copy(level).wait_recv()
            couple(level)

        def level_zero():
            exchange_copy(0).wait_recv()
            couple(0)

        def slot_two(first, last):
            @pl.when(has_behind)
            def _():
                near_slot(2, flags[1], first, last)

        def two():
            points_here(1)
            points_here(2)
            far_level(2)

        work = {}
        for at in range(4):
            work[at] = functools.partial(near_self, at, at + 1)
            work[4 + at] = functools.partial(near_slot, 4, mask[0, 2], at, at + 1)
            work[10 + at] = functools.partial(near_slot, 0, flags[0], at, at + 1)
        work[8] = level_zero
        work[14] = functools.partial(slot_two, 0, 2)
        work[15] = functools.partial(slot_two, 2, 4)
        work[16] = two

        total = 2 * (CHUNKS + 1)
        for at in range(total + LAG):
            if at < total:
                relay(at)
            if at >= LAG:
                collect(at - LAG)
            if at in work:
                work[at]()
        points_here(3)
        far_level(3)
        points_here(4)
        far_level(4)

        @pl.when(has_behind | jnp.logical_not(even))
        def _():
            near_slot(third, flags[2])

        exchange_copy(1).wait_recv()
        share_copy(1).start()
        far_level(1)

    @pl.when(core == 1)
    def _():
        def chain(level):
            bits = reduce_bits(level)
            term_copy(level).wait_recv()
            offset, length = 0, rank

            def incoming(at, start):
                if at == 0:
                    return mx[level, pl.ds(start, length // 2)].astype(F32)
                return rx[level, pl.ds(pl.multiple_of(rank - 2 * length + start, length // 2), length // 2)].astype(F32)

            for at, bit in enumerate(bits):
                shorter = length // 2
                on = partner(bit)[1]
                sent = pl.multiple_of((1 - on) * shorter, shorter)
                kept = pl.multiple_of(on * shorter, shorter)
                there = pl.ds(pl.multiple_of(offset + sent, shorter), shorter)
                here = pl.ds(pl.multiple_of(offset + kept, shorter), shorter)
                tx[level, rank - length : rank - length + shorter] = (
                    keep[level, there] + incoming(at, sent)
                ).astype(BF16)
                reduce_copy(level, at).start()
                keep[level, here] = keep[level, here] + incoming(at, kept)
                offset, length = offset + kept, shorter
                yield
                reduce_copy(level, at).wait()
            last = rx[level, rank - 2 * length : rank - length].astype(F32)
            tx[level, rank - length :] = (
                keep[level, pl.ds(pl.multiple_of(offset, length), length)] + last
            ).astype(BF16)
            exchange_copy(level).start()
            yield
            exchange_copy(level).wait()
            for at in range(len(bits) - 1, -1, -1):
                gather_copy(level, at).start()
                yield
                gather_copy(level, at).wait()
            share_copy(level).start()

        chains = {level: chain(level) for level in range(2, levels)}

        def advance(*which):
            for level in which:
                next(chains[level], None)

        def points_on(level):
            points_copy(level).wait()
            if level:
                points_mate(level).start()
            points_join(level)
            if level + 1 < levels:
                points_copy(level + 1).start()

        keep[4] = term(4)
        keep[3] = term(3)
        advance(4)
        keep[2] = term(2)
        advance(3)
        level_zero_and_one()
        advance(2)
        points_on(0)
        near_self(0, 2)
        advance(4, 3)
        own(1).wait_recv()
        own(0).wait_recv()
        near_self(2, 4)
        advance(2)
        advance(4, 3)
        level_one_ready()
        points_on(1)
        near_slot(4, mask[0, 1], 0, 2)
        advance(4, 3)
        near_slot(4, mask[0, 1], 2, 4)
        points_on(2)
        advance(4, 2)
        exchange_copy(1).start()
        advance(3, 4)
        points_on(3)
        exchange_copy(0).wait_recv()
        couple(0)
        advance(4, 3, 2)
        couple(2)
        couple(3)
        points_on(4)

        flags = [
            mask[0, 2],
            jnp.where(even, mask[0, 3], mask[0, 0]),
            jnp.where(even, mask[0, 0], mask[0, 3]),
        ]

        @pl.when(even)
        def _():
            for chunk in chunks:
                to_mate(0, chunk).wait_recv()

        @pl.when(has_behind & jnp.logical_not(even))
        def _():
            for chunk in chunks:
                to_mate(2, chunk).wait_recv()

        @pl.when(has_behind | even)
        def _():
            near_slot(jnp.where(even, 0, 2), flags[0])

        for chunk in chunks:
            to_mate(1, chunk).wait_recv()
        near_slot(1, flags[1])
        advance(4)
        couple(4)

        @pl.when(has_behind)
        def _():
            for chunk in chunks:
                to_mate(3, chunk).wait_recv()
            near_slot(3, flags[2])

        exchange_copy(1).wait_recv()
        share_copy(1).start()
        share_copy(1).wait_recv()
        couple(1)

    total = far[...].astype(BF16)

    @pl.loop(0, tiles)
    def _(at):
        rows = pl.ds(pl.multiple_of(at * block, block), block)
        out[rows] = (near[rows] + dot(interp[rows], total)).astype(out.dtype)

    own(0).wait_send()
    own(1).wait_send()
    term_copy(1).wait_send()
    exchange_copy(0).wait_send()
    exchange_copy(1).wait_send()
    share_copy(1).wait_send()

    @pl.when(core == 0)
    def _():
        for level in range(2, levels):
            term_copy(level).wait_send()
        for chunk in chunks:
            to_x(0, chunk).wait_send()
            to_x(1, chunk).wait_send()

            @pl.when(has_ahead)
            def _():
                forward(0, chunk).wait_send()
                forward(1, chunk).wait_send()

            to_mate(1, chunk).wait_send()

            @pl.when(even)
            def _():
                to_mate(0, chunk).wait_send()

            @pl.when(has_behind)
            def _():
                to_mate(3, chunk).wait_send()

            @pl.when(has_behind & jnp.logical_not(even))
            def _():
                to_mate(2, chunk).wait_send()

    @pl.when(core == 1)
    def _():
        for level in range(2, levels):
            share_copy(level).wait_send()
        for level in range(1, levels):
            points_mate(level).wait_send()


def per_device(points, weights, interp, transfers, near_mask, skel_index):
    count = lax.axis_size("leaf")
    dim, npts = points.shape
    rhs, rank = weights.shape[1], interp.shape[1]
    levels = transfers.shape[1]
    deep = -(-(dim + 3) // 16) * 16
    slots = plan(levels)
    vmem = pl.BlockSpec(memory_space=pltpu.VMEM)
    return pl.pallas_call(
        functools.partial(body, count, slots),
        out_shape=jax.ShapeDtypeStruct((npts, rhs), BF16),
        in_specs=[vmem] * 4 + [pl.BlockSpec(memory_space=pltpu.SMEM), vmem],
        out_specs=vmem,
        scratch_shapes=[
            pltpu.VMEM((deep, npts), BF16),
            pltpu.VMEM((npts, LANES), BF16),
            pltpu.VMEM((npts, 1), F32),
            pltpu.VMEM((5, deep, npts), BF16),
            pltpu.VMEM((5, npts, rhs), BF16),
            pltpu.VMEM((npts, rhs), F32),
            pltpu.VMEM((rank, rhs), BF16),
            pltpu.VMEM((levels, rank, rhs), F32),
            pltpu.VMEM((levels, rank, rhs), BF16),
            pltpu.VMEM((levels, rank, rhs), BF16),
            pltpu.VMEM((levels, rank, rhs), BF16),
            pltpu.VMEM((levels, rank, rhs), BF16),
            pltpu.VMEM((levels, rank, LANES), BF16),
            pltpu.VMEM((levels, rank, LANES), BF16),
            pltpu.VMEM((rank, rhs), F32),
            pltpu.SemaphoreType.DMA((len(slots),)),
            pltpu.SemaphoreType.DMA((len(slots),)),
        ],
        compiler_params=pltpu.CompilerParams(
            collective_id=0, has_side_effects=True, vmem_limit_bytes=60 * 2**20
        ),
    )(points, weights, interp, transfers[0], near_mask, skel_index)


def solution(mesh):
    return jax.shard_map(
        per_device,
        mesh=mesh,
        in_specs=(
            P(None, "leaf"),
            P("leaf", None),
            P("leaf", None),
            P("leaf", None, None, None),
            P("leaf", None),
            P("leaf", None),
        ),
        out_specs=P("leaf", None),
        check_vma=False,
    )
```
